32 devices in a mesh: ens: 2 (over x), row: 4 (over z), col: 4 (over y, core).
Axes of the slice: x: 2, y: 2, z: 4, core: 2. Of those that a mesh axis runs over, the one named last changes fastest.
Arguments:
- adjoint: float32 [2, 3, 8, 512, 2048], P('ens', None, 'col', 'row'), may hold values from -6 to 6
- base_flow: float32 [2, 2, 8, 512, 2048], P('ens', None, 'col', 'row'), may hold values from -6 to 6
- stream_first: float32 [16, 128, 128], replicated, may hold values from -0.125 to 0.125
- stream_second: float32 [16, 128, 128], replicated, may hold values from -0.125 to 0.125
- wall_first: float32 [512, 512], replicated, may hold values from -0.25 to 0.25
- wall_second: float32 [512, 512], replicated, may hold values from -0.25 to 0.25
- forcing: float32 [3, 8, 512, 2048], P(None, 'col', 'row'), may hold values from 0.3 to 3
Outputs:
- updated: float32 [2, 3, 8, 512, 2048], P('ens', None, 'col', 'row')
- gradient: float32 [3, 8, 512, 2048], P(None, 'col', 'row')
The draws below stay inside these ranges and needn't reach their ends.
All inputs are finite; a program needn't handle non-finite values.
Results may differ from the reference program's by a relative error of at most 0.000071.
Values sent between devices are 32-bit elements; how exact they have to be, the bound alone decides.
A program may use at most 384 MiB of HBM per device.

```python
import math
import jax
import jax.numpy as jnp
from jax import lax

NX = 2048
NY = 512
BLK = 128
NBX = 16
NZ = 8
MEMBERS = 2


def block_levels(rng, shape, cuts, smallest, largest):
    factor_of = 1.0
    for dim, shards_of in cuts:
        draws = jax.random.uniform(jax.random.fold_in(jax.random.fold_in(rng, 6), dim), (shards_of,), jnp.float32, smallest / len(cuts), largest / len(cuts))
        factor_of = factor_of * jnp.repeat(jnp.exp(draws), shape[dim] // shards_of).reshape((-1,) + (1,) * (len(shape) - 1 - dim))
    return factor_of


def bell_draw(own_key, dims, scale, most, cuts=(), held_as=jnp.bfloat16):
    values = scale * jax.random.normal(own_key, dims, jnp.float32)
    if cuts:
        values = values * block_levels(own_key, dims, cuts, -0.22, 0.18)
    return jnp.clip(values, -most, most).astype(held_as)


def setup_inputs(seed: int = 0) -> dict:
    key_of = jax.random.split(jax.random.key(seed), 8)
    adjoint = bell_draw(key_of[0], (MEMBERS, 3, NZ, NY, NX), 1.0, 6.0, ((0, 2), (2, 4), (3, 4)), jnp.float32)
    base_flow = bell_draw(key_of[1], (MEMBERS, 2, NZ, NY, NX), 1.0, 6.0, ((0, 2), (2, 4), (3, 4)), jnp.float32)
    stream_first = bell_draw(key_of[2], (NBX, BLK, BLK), NX ** -0.5, 0.125, (), jnp.float32)
    stream_second = bell_draw(key_of[3], (NBX, BLK, BLK), NX ** -0.5, 0.125, (), jnp.float32)
    wall_first = bell_draw(key_of[4], (NY, NY), NY ** -0.5, 0.25, (), jnp.float32)
    wall_second = bell_draw(key_of[5], (NY, NY), NY ** -0.5, 0.25, (), jnp.float32)
    forcing = jnp.clip(jnp.exp(math.log(3.0) - 2.3025851 * jax.random.uniform(key_of[6], (3, NZ, NY, NX), jnp.float32) ** block_levels(key_of[6], (3, NZ, NY, NX), ((1, 4), (2, 4)), -0.2, 0.2)), 0.3, 3.0)
    return {"adjoint": adjoint, "base_flow": base_flow, "stream_first": stream_first, "stream_second": stream_second, "wall_first": wall_first, "wall_second": wall_second, "forcing": forcing}


viscosity = 0.5
step_weight = 0.25


def circulant(blocks):
    block_count = blocks.shape[0]
    block_size = blocks.shape[1]
    rows_index = jnp.arange(block_count, dtype=jnp.int32)
    offsets = ((rows_index[None, :] - rows_index[:, None]) % block_count).astype(jnp.int32)
    tiled = blocks[offsets]
    return tiled.transpose(0, 2, 1, 3).reshape(block_count * block_size, block_count * block_size)


def along_stream(values, operator):
    return jnp.einsum('...j,ij->...i', values, operator, precision=lax.Precision.HIGHEST)


def along_wall(values, operator):
    return jnp.einsum('ky,...yx->...kx', operator, values, precision=lax.Precision.HIGHEST)


def reference(adjoint, base_flow, stream_first, stream_second, wall_first, wall_second, forcing):
    dense_first = circulant(stream_first)
    dense_second = circulant(stream_second)

    def member(pair):
        adj_field, base_speed = pair
        x_first = along_stream(adj_field, dense_first)
        x_second = along_stream(adj_field, dense_second)
        rhs_stream = viscosity * x_second + base_speed[0:1] * x_first
        y_first = along_wall(adj_field, wall_first)
        y_second = along_wall(adj_field, wall_second)
        rhs_wall = viscosity * y_second + base_speed[1:2] * y_first
        return adj_field + step_weight * (rhs_stream + rhs_wall)

    updated = lax.map(member, (adjoint, base_flow))
    gradient = forcing * jnp.sum(updated, axis=0)
    return updated, gradient
```

```python
import functools
import math

import jax
import jax.numpy as jnp
from jax import lax
from jax.experimental import pallas as pl
from jax.experimental.pallas import tpu as pltpu
from jax.sharding import PartitionSpec as P

viscosity = 0.5
step_weight = 0.25
MESH = pl.DeviceIdType.MESH
TILE = 256


def split(v):
    hi = v.astype(jnp.bfloat16)
    return hi, (v - hi.astype(jnp.float32)).astype(jnp.bfloat16)


def turn(re, im, angle):
    c, s = math.cos(angle), math.sin(angle)
    if abs(s) < 1e-12 and c > 0:
        return re, im
    if abs(c) < 1e-12:
        if s < 0:
            return im, (-re if re is not None else None)
        return (-im if im is not None else None), re
    if im is None:
        return re * c, re * s
    return re * c - im * s, re * s + im * c


def plus(a, b):
    if a is None:
        return b
    return a if b is None else a + b


def minus(a, b):
    if b is None:
        return a
    return -b if a is None else a - b


def real_dft(xs):
    n = len(xs)
    if n == 2:
        return [(xs[0] + xs[1], None), (xs[0] - xs[1], None)]
    even, odd = real_dft(xs[0::2]), real_dft(xs[1::2])
    out = [None] * (n // 2 + 1)
    for k in range(n // 4 + 1):
        er, ei = even[k]
        tr, ti = turn(odd[k][0], odd[k][1], -2 * math.pi * k / n)
        out[k] = (plus(er, tr), plus(ei, ti))
        if k != n // 4:
            dr, di = minus(er, tr), minus(ei, ti)
            out[n // 2 - k] = (dr, None if di is None else -di)
    return out


def real_idft(ys):
    n = 2 * (len(ys) - 1)
    if n == 2:
        return [ys[0][0] + ys[1][0], ys[0][0] - ys[1][0]]
    even, odd = [], []
    for k in range(n // 4 + 1):
        ar, ai = ys[k]
        br, bi = ys[n // 2 - k]
        if k == n // 4:
            even.append((ar + ar, None))
            dr, di = None, None if ai is None else ai + ai
        else:
            even.append((ar + br, minus(ai, bi)))
            dr, di = ar - br, plus(ai, bi)
        odd.append(turn(dr, di, 2 * math.pi * k / n))
    for part in (even, odd):
        part[0] = (part[0][0], None)
        part[-1] = (part[-1][0], None)
    e, o = real_idft(even), real_idft(odd)
    out = [None] * n
    out[0::2], out[1::2] = e, o
    return out


def dot_last(a, b):
    return lax.dot_general(a, b, (((1,), (1,)), ((), ())), preferred_element_type=jnp.float32)


def dot(a, b):
    return jnp.dot(a, b, preferred_element_type=jnp.float32)


def kernel(
    units, nz, adj, base, sf_in, ss_in, wf_in, ws_in, forcing, upd_out, grad_out,
    sf, ss, wf, ws,
    own, part, mid, far, flow, flow_in, acc, other, gh, gl, xh, xl, yb, wh, wl, ch, cl,
    s1, r1, s2, r2, s3, r3, s4, r4, s5, r5, sb, rb, la, lb, lf, ou, og, lw,
):
    nc, ny, nx = own.shape
    nb, blk, _ = sf.shape
    half = nb // 2
    nu = len(units)
    e, r = lax.axis_index("ens"), lax.axis_index("row")
    near, across = r ^ 1, r ^ 3
    outer = jnp.logical_or(r == 0, r == 3)
    inner = jnp.logical_not(outer)

    def at(ref, u):
        c, x0, w = units[u]
        return ref.at[c, :, pl.ds(x0, w)]

    def send(src, dst, ssem, rsem, where):
        return pltpu.make_async_remote_copy(
            src_ref=src, dst_ref=dst, send_sem=ssem, recv_sem=rsem,
            device_id=where, device_id_type=MESH)

    def c1(u):
        return send(at(adj, u), at(part, u), s1.at[u], r1.at[u], {"row": near})

    def cb(z):
        return send(base.at[nz + z], flow_in.at[z], sb.at[z], rb.at[z], {"row": near})

    def c2(u):
        return send(at(adj, u), at(mid, u), s2.at[u], r2.at[u], {"row": across})

    def c3(u):
        return send(at(part, u), at(far, u), s3.at[u], r3.at[u], {"row": across})

    def c4(u):
        return send(at(own, u), at(far, u), s4.at[u], r4.at[u], {"row": near})

    def c5(u):
        return send(at(acc, u), at(other, u), s5.at[u], r5.at[u], {"ens": 1 - e})

    def load_adj(c):
        return pltpu.make_async_copy(adj.at[c], own.at[c], la.at[c])

    def load_flow():
        return pltpu.make_async_copy(base, flow, lb)

    def load_forcing(u):
        return pltpu.make_async_copy(at(forcing, u), at(mid, u), lf.at[u])

    def put_upd(u):
        return pltpu.make_async_copy(at(acc, u), at(upd_out, u), ou.at[u])

    def put_grad(u):
        return pltpu.make_async_copy(at(other, u), at(grad_out, u), og.at[u])

    barrier = pltpu.get_barrier_semaphore()
    for where in ({"row": near}, {"row": across}, {"ens": 1 - e}):
        pl.semaphore_signal(barrier, inc=1, device_id=where, device_id_type=MESH)
    pl.semaphore_wait(barrier, 3)

    ahead = min(2, nu)
    reach = min(2, nu - 1)
    lag = min(4, nu)
    order_z = []
    for c, _, _ in units:
        if c % nz not in order_z:
            order_z.append(c % nz)

    @pl.when(outer)
    def _():
        due = {}
        for z in order_z:
            first = min(u for u in range(nu) if units[u][0] % nz == z)
            due.setdefault(min(first + (2 if first == 0 else 0), nu - 1), []).append(z)
        for u in range(nu):
            c1(u).start()
            for z in due.get(u, ()):
                cb(z).start()

    @pl.when(inner)
    def _():
        for u in range(ahead):
            c2(u).start()

    def load_operators():
        pairs = ((sf_in, sf), (ss_in, ss), (wf_in, wf), (ws_in, ws))
        return [pltpu.make_async_copy(a, b, lw.at[i]) for i, (a, b) in enumerate(pairs)]

    for copy in load_operators():
        copy.start()
    for c in range(nc):
        load_adj(c).start()
    load_flow().start()

    for copy in load_operators():
        copy.wait()

    gh[0] = jnp.zeros(gh.shape[1:], gh.dtype)
    gl[0] = jnp.zeros(gl.shape[1:], gl.dtype)

    @pl.loop(0, blk // 16)
    def _(i):
        rows = pl.multiple_of(i * 16, 16)
        for o, (ref, scale) in enumerate(((sf, step_weight), (ss, step_weight * viscosity))):
            xs = [ref[m, pl.ds(rows, 16), :] * (scale / nb) for m in range(nb)]
            fs = real_dft(xs)

            def keep(k, out_half, in_half, v):
                hi, lo = split(v)
                dst = pl.ds(rows + (2 * o + out_half) * blk, 16)
                cols = slice(in_half * blk, (in_half + 1) * blk)
                gh[k, dst, cols] = hi
                gl[k, dst, cols] = lo

            keep(0, 0, 0, fs[0][0])
            keep(0, 1, 1, fs[half][0])
            for k in range(1, half):
                cr, ci = fs[k]
                keep(k, 0, 0, cr)
                keep(k, 0, 1, ci)
                keep(k, 1, 0, -ci)
                keep(k, 1, 1, cr)

    for a, ro in enumerate((r, near)):
        for o, (ref, scale) in enumerate(((wf, step_weight), (ws, step_weight * viscosity))):
            for b, co in enumerate((r, near, across, r ^ 2)):
                v = ref[pl.ds(pl.multiple_of(ro * ny, 128), ny), pl.ds(pl.multiple_of(co * ny, 128), ny)] * scale
                hi, lo = split(v)
                i = 2 * a + o
                wh[i * ny:(i + 1) * ny, b * ny:(b + 1) * ny] = hi
                wl[i * ny:(i + 1) * ny, b * ny:(b + 1) * ny] = lo

    load_flow().wait()

    def stream(c):
        load_adj(c).wait()

        @pl.loop(0, ny // 16)
        def _(i):
            rows = pl.ds(pl.multiple_of(i * 16, 16), 16)
            fs = real_dft([own[c, rows, p * blk:(p + 1) * blk] for p in range(nb)])
            for k in range(half):
                pair = (fs[0][0], fs[half][0]) if k == 0 else fs[k]
                for t in range(2):
                    hi, lo = split(pair[t])
                    at_col = (2 * k + t) * blk
                    xh[rows, at_col:at_col + blk] = hi
                    xl[rows, at_col:at_col + blk] = lo

        @pl.loop(0, half)
        def _(k):
            cols = pl.ds(pl.multiple_of(k * 2 * blk, 128), 2 * blk)
            hi, lo = xh[:, cols], xl[:, cols]
            yb[k] = dot_last(hi, gh[k]) + (dot_last(hi, gl[k]) + dot_last(lo, gh[k]))

        @pl.loop(0, ny // 8)
        def _(i):
            rows = pl.ds(pl.multiple_of(i * 8, 8), 8)
            for o in range(2):
                b0 = 2 * o * blk
                ys = [(yb[0, rows, b0:b0 + blk], None)]
                for k in range(1, half):
                    ys.append((yb[k, rows, b0:b0 + blk], yb[k, rows, b0 + blk:b0 + 2 * blk]))
                ys.append((yb[0, rows, b0 + blk:b0 + 2 * blk], None))
                xs = real_idft(ys)
                for p in range(nb):
                    cols = slice(p * blk, (p + 1) * blk)
                    if o == 0:
                        acc[c, rows, cols] = own[c, rows, cols] + flow[c % nz, rows, cols] * xs[p]
                    else:
                        acc[c, rows, cols] = acc[c, rows, cols] + xs[p]

    def wall(u):
        c, x0, w = units[u]
        z = c % nz

        tile = min(TILE, w)

        @pl.loop(0, w // tile)
        def _(t):
            cols = pl.ds(pl.multiple_of(x0 + t * tile, 128), tile)
            for b, ref in enumerate((own, part, mid, far)):
                hi, lo = split(ref[c, :, cols])
                ch[b * ny:(b + 1) * ny, :tile] = hi
                cl[b * ny:(b + 1) * ny, :tile] = lo
            hi, lo = ch[:, :tile], cl[:, :tile]
            y = dot(wh[...], hi) + (dot(wh[...], lo) + dot(wl[...], hi))
            acc[c, :, cols] = acc[c, :, cols] + (y[ny:2 * ny] + flow[nz + z, :, cols] * y[:ny])
            own[c, :, cols] = y[3 * ny:] + flow_in[z, :, cols] * y[2 * ny:3 * ny]

    def add_wall(u):
        c, x0, w = units[u]

        @pl.loop(0, ny // 8)
        def _(i):
            rows = pl.ds(pl.multiple_of(i * 8, 8), 8)
            cols = slice(x0, x0 + w)
            acc[c, rows, cols] = acc[c, rows, cols] + far[c, rows, cols]

    def gradient(u):
        c, x0, w = units[u]
        c5(u).wait_recv()
        load_forcing(u).wait()

        @pl.loop(0, ny // 8)
        def _(i):
            rows = pl.ds(pl.multiple_of(i * 8, 8), 8)
            cols = slice(x0, x0 + w)
            other[c, rows, cols] = mid[c, rows, cols] * (acc[c, rows, cols] + other[c, rows, cols])

        put_grad(u).start()

    done = set()

    turns = []
    for c, _, _ in units:
        if c not in turns:
            turns.append(c)

    def need(i):
        c = turns[min(i, nc - 1)]
        if c not in done:
            done.add(c)
            stream(c)

    big = max(u for u in range(nu) if units[u][2] == units[0][2])

    def due_mid(u):
        return max(min(u + ahead + 1, big + 1), min(u + 2, nu))

    def due_relay(u):
        return nu if u >= big - 1 else min(u + 1 + reach, nu)

    def relay(u):
        @pl.when(inner)
        def _():
            c1(u).wait_recv()
            c3(u).start()
            for v in range(due_mid(u - 1), due_mid(u)):
                c2(v).start()

    waited = set()
    need(0)
    for u in range(due_relay(-1)):
        relay(u)
    need(1)
    for u in range(nu):
        for v in range(due_relay(u - 1), due_relay(u)):
            relay(v)
        c = units[u][0]
        need(turns.index(c))
        need(turns.index(c) + 1)
        z = c % nz
        first = z not in waited
        waited.add(z)

        @pl.when(inner)
        def _():
            if first:
                cb(z).wait_recv()
            c2(u).wait_recv()
            c3(u).wait_recv()
            wall(u)
            c4(u).start()

        @pl.when(outer)
        def _():
            c4(u).wait_recv()
            add_wall(u)

        c5(u).start()
        put_upd(u).start()
        load_forcing(u).start()
        if u >= lag:
            gradient(u - lag)
    for u in range(nu - lag, nu):
        gradient(u)

    @pl.when(outer)
    def _():
        for u in range(nu):
            c1(u).wait_send()
        for z in order_z:
            cb(z).wait_send()

    @pl.when(inner)
    def _():
        for u in range(nu):
            c2(u).wait_send()
            c3(u).wait_send()
            c4(u).wait_send()

    for u in range(nu):
        c5(u).wait_send()
        put_upd(u).wait()
        put_grad(u).wait()


def fused(adjoint, base_flow, stream_first, stream_second, wall_first, wall_second, forcing):
    _, nf, nz, ny, nx = adjoint.shape
    nc = nf * nz
    nb, blk, _ = stream_first.shape
    units, turns = [], []
    for c in [f * nz + z for z in range(nz) for f in range(nf)]:
        widths = [nx // 2, nx // 2]
        if len(turns) == nc - 2:
            widths = [nx // 2, nx // 4, nx // 4]
        if len(turns) == nc - 1:
            widths = [nx // 4] + [nx // 8] * 5 + [nx // 16] * 2
        turns.append(c)
        x0 = 0
        for w in widths:
            units.append((c, x0, w))
            x0 += w
    nu = len(units)
    f32, bf16 = jnp.float32, jnp.bfloat16
    field = pltpu.VMEM((nc, ny, nx), f32)
    n_ops = 4 * ny
    dma = pltpu.SemaphoreType.DMA
    any_spec = pl.BlockSpec(memory_space=pl.ANY)
    updated, gradient = pl.pallas_call(
        functools.partial(kernel, tuple(units), nz),
        out_shape=(jax.ShapeDtypeStruct((nc, ny, nx), f32), jax.ShapeDtypeStruct((nc, ny, nx), f32)),
        in_specs=[any_spec] * 7,
        out_specs=(any_spec, any_spec),
        scratch_shapes=[pltpu.VMEM(a.shape, f32) for a in (stream_first, stream_second, wall_first, wall_second)] + [
            field, field, field, field,
            pltpu.VMEM((2 * nz, ny, nx), f32), pltpu.VMEM((nz, ny, nx), f32),
            field, field,
            pltpu.VMEM((nb // 2, 4 * blk, 2 * blk), bf16), pltpu.VMEM((nb // 2, 4 * blk, 2 * blk), bf16),
            pltpu.VMEM((ny, nx), bf16), pltpu.VMEM((ny, nx), bf16),
            pltpu.VMEM((nb // 2, ny, 4 * blk), f32),
            pltpu.VMEM((n_ops, 4 * ny), bf16), pltpu.VMEM((n_ops, 4 * ny), bf16),
            pltpu.VMEM((4 * ny, TILE), bf16), pltpu.VMEM((4 * ny, TILE), bf16),
        ] + [dma((nu,))] * 10 + [dma((nz,))] * 2 + [dma((nc,)), dma, dma((nu,)), dma((nu,)), dma((nu,)), dma((4,))],
        compiler_params=pltpu.CompilerParams(
            collective_id=0, has_side_effects=True, vmem_limit_bytes=67043328),
    )(
        adjoint.reshape(nc, ny, nx), base_flow.reshape(-1, ny, nx),
        stream_first, stream_second, wall_first, wall_second, forcing.reshape(nc, ny, nx),
    )
    return updated.reshape(adjoint.shape), gradient.reshape(forcing.shape)


def stream_terms(adj_field, stream_first, stream_second):
    block_count = stream_first.shape[0]
    block_size = stream_first.shape[1]
    blocks_view = adj_field.reshape(-1, block_count, block_size)
    first_sum = jnp.zeros(blocks_view.shape, jnp.float32)
    second_sum = jnp.zeros(blocks_view.shape, jnp.float32)
    for shift_count in range(block_count):
        shifted = jnp.roll(blocks_view, -shift_count, axis=1)
        first_sum = first_sum + jnp.einsum(
            "mpj,ij->mpi", shifted, stream_first[shift_count], precision=lax.Precision.HIGHEST
        )
        second_sum = second_sum + jnp.einsum(
            "mpj,ij->mpi", shifted, stream_second[shift_count], precision=lax.Precision.HIGHEST
        )
    return (first_sum.reshape(adj_field.shape), second_sum.reshape(adj_field.shape))


def local(adjoint, base_flow, stream_first, stream_second, wall_first, wall_second, forcing):
    adj_field = adjoint[0]
    base_speed = base_flow[0]
    x_first, x_second = stream_terms(adj_field, stream_first, stream_second)
    rhs_stream = viscosity * x_second + base_speed[0:1] * x_first
    lines = lax.all_to_all(adj_field, "row", split_axis=3, concat_axis=2, tiled=True)
    y_first = jnp.einsum("ky,fzyx->fzkx", wall_first, lines, precision=lax.Precision.HIGHEST)
    y_second = jnp.einsum("ky,fzyx->fzkx", wall_second, lines, precision=lax.Precision.HIGHEST)
    y_first, y_second = (y_first, y_second)
    y_first, y_second = (
        lax.all_to_all(y_first, "row", split_axis=2, concat_axis=3, tiled=True),
        lax.all_to_all(y_second, "row", split_axis=2, concat_axis=3, tiled=True),
    )
    rhs_wall = viscosity * y_second + base_speed[1:2] * y_first
    updated = adj_field + step_weight * (rhs_stream + rhs_wall)
    summed = lax.psum(updated, "ens")
    gradient = forcing * summed
    return (updated[None], gradient)


def solution(mesh):
    placed = (
        P("ens", None, "col", "row", None),
        P("ens", None, "col", "row", None),
        P(),
        P(),
        P(),
        P(),
        P(None, "col", "row", None),
    )
    small = mesh.shape["row"] == 4 and mesh.shape["ens"] == 2
    return jax.shard_map(
        fused if small else local,
        mesh=mesh,
        in_specs=placed,
        out_specs=(P("ens", None, "col", "row", None), P(None, "col", "row", None)),
        check_vma=False,
    )
```

```python
import functools
import math

import jax
import jax.numpy as jnp
from jax import lax
from jax.experimental import pallas as pl
from jax.experimental.pallas import tpu as pltpu
from jax.sharding import PartitionSpec as P

viscosity = 0.5
step_weight = 0.25
MESH = pl.DeviceIdType.MESH
TILE = 256


def split(v):
    hi = v.astype(jnp.bfloat16)
    return hi, (v - hi.astype(jnp.float32)).astype(jnp.bfloat16)


def turn(re, im, angle):
    c, s = math.cos(angle), math.sin(angle)
    if abs(s) < 1e-12 and c > 0:
        return re, im
    if abs(c) < 1e-12:
        if s < 0:
            return im, (-re if re is not None else None)
        return (-im if im is not None else None), re
    if im is None:
        return re * c, re * s
    return re * c - im * s, re * s + im * c


def plus(a, b):
    if a is None:
        return b
    return a if b is None else a + b


def minus(a, b):
    if b is None:
        return a
    return -b if a is None else a - b


def real_dft(xs):
    n = len(xs)
    if n == 2:
        return [(xs[0] + xs[1], None), (xs[0] - xs[1], None)]
    even, odd = real_dft(xs[0::2]), real_dft(xs[1::2])
    out = [None] * (n // 2 + 1)
    for k in range(n // 4 + 1):
        er, ei = even[k]
        tr, ti = turn(odd[k][0], odd[k][1], -2 * math.pi * k / n)
        out[k] = (plus(er, tr), plus(ei, ti))
        if k != n // 4:
            dr, di = minus(er, tr), minus(ei, ti)
            out[n // 2 - k] = (dr, None if di is None else -di)
    return out


def real_idft(ys):
    n = 2 * (len(ys) - 1)
    if n == 2:
        return [ys[0][0] + ys[1][0], ys[0][0] - ys[1][0]]
    even, odd = [], []
    for k in range(n // 4 + 1):
        ar, ai = ys[k]
        br, bi = ys[n // 2 - k]
        if k == n // 4:
            even.append((ar + ar, None))
            dr, di = None, None if ai is None else ai + ai
        else:
            even.append((ar + br, minus(ai, bi)))
            dr, di = ar - br, plus(ai, bi)
        odd.append(turn(dr, di, 2 * math.pi * k / n))
    for part in (even, odd):
        part[0] = (part[0][0], None)
        part[-1] = (part[-1][0], None)
    e, o = real_idft(even), real_idft(odd)
    out = [None] * n
    out[0::2], out[1::2] = e, o
    return out


def dot_last(a, b):
    return lax.dot_general(a, b, (((1,), (1,)), ((), ())), preferred_element_type=jnp.float32)


def dot(a, b):
    return jnp.dot(a, b, preferred_element_type=jnp.float32)


def kernel(
    units, nz, adj, base, sf_in, ss_in, wf_in, ws_in, forcing, acc, other,
    sf, ss, wf, ws,
    own, part, mid, far, flow, flow_in, gh, gl, xh, xl, yb, wh, wl, ch, cl,
    s1, r1, s2, r2, s3, r3, s4, r4, s5, r5, sb, rb, la, lb, lf, lw,
):
    nc, ny, nx = own.shape
    nb, blk, _ = sf.shape
    half = nb // 2
    nu = len(units)
    e, r = lax.axis_index("ens"), lax.axis_index("row")
    near, across = r ^ 1, r ^ 3
    outer = jnp.logical_or(r == 0, r == 3)
    inner = jnp.logical_not(outer)

    def at(ref, u):
        c, x0, w = units[u]
        return ref.at[c, :, pl.ds(x0, w)]

    def send(src, dst, ssem, rsem, where):
        return pltpu.make_async_remote_copy(
            src_ref=src, dst_ref=dst, send_sem=ssem, recv_sem=rsem,
            device_id=where, device_id_type=MESH)

    def c1(u):
        return send(at(adj, u), at(part, u), s1.at[u], r1.at[u], {"row": near})

    def cb(z):
        return send(base.at[nz + z], flow_in.at[z], sb.at[z], rb.at[z], {"row": near})

    def c2(u):
        return send(at(adj, u), at(mid, u), s2.at[u], r2.at[u], {"row": across})

    def c3(u):
        return send(at(part, u), at(far, u), s3.at[u], r3.at[u], {"row": across})

    def c4(u):
        return send(at(own, u), at(far, u), s4.at[u], r4.at[u], {"row": near})

    def c5(u):
        return send(at(acc, u), at(other, u), s5.at[u], r5.at[u], {"ens": 1 - e})

    def load_adj(c):
        return pltpu.make_async_copy(adj.at[c], own.at[c], la.at[c])

    def load_flow():
        return pltpu.make_async_copy(base, flow, lb)

    def load_forcing(u):
        return pltpu.make_async_copy(at(forcing, u), at(mid, u), lf.at[u])

    barrier = pltpu.get_barrier_semaphore()
    for where in ({"row": near}, {"row": across}, {"ens": 1 - e}):
        pl.semaphore_signal(barrier, inc=1, device_id=where, device_id_type=MESH)
    pl.semaphore_wait(barrier, 3)

    ahead = min(2, nu)
    reach = min(2, nu - 1)
    lag = min(4, nu)
    order_z = []
    for c, _, _ in units:
        if c % nz not in order_z:
            order_z.append(c % nz)

    @pl.when(outer)
    def _():
        due = {}
        for z in order_z:
            first = min(u for u in range(nu) if units[u][0] % nz == z)
            due.setdefault(min(first + (2 if first == 0 else 0), nu - 1), []).append(z)
        for u in range(nu):
            c1(u).start()
            for z in due.get(u, ()):
                cb(z).start()

    @pl.when(inner)
    def _():
        for u in range(ahead):
            c2(u).start()

    def load_operators():
        pairs = ((sf_in, sf), (ss_in, ss), (wf_in, wf), (ws_in, ws))
        return [pltpu.make_async_copy(a, b, lw.at[i]) for i, (a, b) in enumerate(pairs)]

    for copy in load_operators():
        copy.start()
    for c in range(nc):
        load_adj(c).start()
    load_flow().start()

    for copy in load_operators():
        copy.wait()

    gh[0] = jnp.zeros(gh.shape[1:], gh.dtype)
    gl[0] = jnp.zeros(gl.shape[1:], gl.dtype)

    @pl.loop(0, blk // 16)
    def _(i):
        rows = pl.multiple_of(i * 16, 16)
        for o, (ref, scale) in enumerate(((sf, step_weight), (ss, step_weight * viscosity))):
            xs = [ref[m, pl.ds(rows, 16), :] * (scale / nb) for m in range(nb)]
            fs = real_dft(xs)

            def keep(k, out_half, in_half, v):
                hi, lo = split(v)
                dst = pl.ds(rows + (2 * o + out_half) * blk, 16)
                cols = slice(in_half * blk, (in_half + 1) * blk)
                gh[k, dst, cols] = hi
                gl[k, dst, cols] = lo

            keep(0, 0, 0, fs[0][0])
            keep(0, 1, 1, fs[half][0])
            for k in range(1, half):
                cr, ci = fs[k]
                keep(k, 0, 0, cr)
                keep(k, 0, 1, ci)
                keep(k, 1, 0, -ci)
                keep(k, 1, 1, cr)

    for a, ro in enumerate((r, near)):
        for o, (ref, scale) in enumerate(((wf, step_weight), (ws, step_weight * viscosity))):
            for b, co in enumerate((r, near, across, r ^ 2)):
                v = ref[pl.ds(pl.multiple_of(ro * ny, 128), ny), pl.ds(pl.multiple_of(co * ny, 128), ny)] * scale
                hi, lo = split(v)
                i = 2 * a + o
                wh[i * ny:(i + 1) * ny, b * ny:(b + 1) * ny] = hi
                wl[i * ny:(i + 1) * ny, b * ny:(b + 1) * ny] = lo

    load_flow().wait()

    def stream(c):
        load_adj(c).wait()

        @pl.loop(0, ny // 16)
        def _(i):
            rows = pl.ds(pl.multiple_of(i * 16, 16), 16)
            fs = real_dft([own[c, rows, p * blk:(p + 1) * blk] for p in range(nb)])
            for k in range(half):
                pair = (fs[0][0], fs[half][0]) if k == 0 else fs[k]
                for t in range(2):
                    hi, lo = split(pair[t])
                    at_col = (2 * k + t) * blk
                    xh[rows, at_col:at_col + blk] = hi
                    xl[rows, at_col:at_col + blk] = lo

        @pl.loop(0, half)
        def _(k):
            cols = pl.ds(pl.multiple_of(k * 2 * blk, 128), 2 * blk)
            hi, lo = xh[:, cols], xl[:, cols]
            yb[k] = dot_last(hi, gh[k]) + (dot_last(hi, gl[k]) + dot_last(lo, gh[k]))

        @pl.loop(0, ny // 8)
        def _(i):
            rows = pl.ds(pl.multiple_of(i * 8, 8), 8)
            for o in range(2):
                b0 = 2 * o * blk
                ys = [(yb[0, rows, b0:b0 + blk], None)]
                for k in range(1, half):
                    ys.append((yb[k, rows, b0:b0 + blk], yb[k, rows, b0 + blk:b0 + 2 * blk]))
                ys.append((yb[0, rows, b0 + blk:b0 + 2 * blk], None))
                xs = real_idft(ys)
                for p in range(nb):
                    cols = slice(p * blk, (p + 1) * blk)
                    if o == 0:
                        acc[c, rows, cols] = own[c, rows, cols] + flow[c % nz, rows, cols] * xs[p]
                    else:
                        acc[c, rows, cols] = acc[c, rows, cols] + xs[p]

    def wall(u):
        c, x0, w = units[u]
        z = c % nz

        tile = min(TILE, w)

        @pl.loop(0, w // tile)
        def _(t):
            cols = pl.ds(pl.multiple_of(x0 + t * tile, 128), tile)
            for b, ref in enumerate((own, part, mid, far)):
                hi, lo = split(ref[c, :, cols])
                ch[b * ny:(b + 1) * ny, :tile] = hi
                cl[b * ny:(b + 1) * ny, :tile] = lo
            hi, lo = ch[:, :tile], cl[:, :tile]
            y = dot(wh[...], hi) + (dot(wh[...], lo) + dot(wl[...], hi))
            acc[c, :, cols] = acc[c, :, cols] + (y[ny:2 * ny] + flow[nz + z, :, cols] * y[:ny])
            own[c, :, cols] = y[3 * ny:] + flow_in[z, :, cols] * y[2 * ny:3 * ny]

    def add_wall(u):
        c, x0, w = units[u]

        @pl.loop(0, ny // 8)
        def _(i):
            rows = pl.ds(pl.multiple_of(i * 8, 8), 8)
            cols = slice(x0, x0 + w)
            acc[c, rows, cols] = acc[c, rows, cols] + far[c, rows, cols]

    def gradient(u):
        c, x0, w = units[u]
        c5(u).wait_recv()
        load_forcing(u).wait()

        @pl.loop(0, ny // 8)
        def _(i):
            rows = pl.ds(pl.multiple_of(i * 8, 8), 8)
            cols = slice(x0, x0 + w)
            other[c, rows, cols] = mid[c, rows, cols] * (acc[c, rows, cols] + other[c, rows, cols])

    done = set()

    turns = []
    for c, _, _ in units:
        if c not in turns:
            turns.append(c)

    def need(i):
        c = turns[min(i, nc - 1)]
        if c not in done:
            done.add(c)
            stream(c)

    big = max(u for u in range(nu) if units[u][2] == units[0][2])

    def due_mid(u):
        return max(min(u + ahead + 1, big + 1), min(u + 2, nu))

    def due_relay(u):
        return nu if u >= big - 1 else min(u + 1 + reach, nu)

    def relay(u):
        @pl.when(inner)
        def _():
            c1(u).wait_recv()
            c3(u).start()
            for v in range(due_mid(u - 1), due_mid(u)):
                c2(v).start()

    waited = set()
    need(0)
    for u in range(due_relay(-1)):
        relay(u)
    need(1)
    for u in range(nu):
        for v in range(due_relay(u - 1), due_relay(u)):
            relay(v)
        c = units[u][0]
        need(turns.index(c))
        need(turns.index(c) + 1)
        z = c % nz
        first = z not in waited
        waited.add(z)

        @pl.when(inner)
        def _():
            if first:
                cb(z).wait_recv()
            c2(u).wait_recv()
            c3(u).wait_recv()
            wall(u)
            c4(u).start()

        @pl.when(outer)
        def _():
            c4(u).wait_recv()
            add_wall(u)

        c5(u).start()
        load_forcing(u).start()
        if u >= lag:
            gradient(u - lag)
    for u in range(nu - lag, nu):
        gradient(u)

    @pl.when(outer)
    def _():
        for u in range(nu):
            c1(u).wait_send()
        for z in order_z:
            cb(z).wait_send()

    @pl.when(inner)
    def _():
        for u in range(nu):
            c2(u).wait_send()
            c3(u).wait_send()
            c4(u).wait_send()

    for u in range(nu):
        c5(u).wait_send()


def fused(adjoint, base_flow, stream_first, stream_second, wall_first, wall_second, forcing):
    _, nf, nz, ny, nx = adjoint.shape
    nc = nf * nz
    nb, blk, _ = stream_first.shape
    units, turns = [], []
    for c in [f * nz + z for z in range(nz) for f in range(nf)]:
        widths = [nx // 2, nx // 2]
        if len(turns) == nc - 2:
            widths = [nx // 2, nx // 4, nx // 4]
        if len(turns) == nc - 1:
            widths = [nx // 4] + [nx // 8] * 5 + [nx // 16] * 2
        turns.append(c)
        x0 = 0
        for w in widths:
            units.append((c, x0, w))
            x0 += w
    nu = len(units)
    f32, bf16 = jnp.float32, jnp.bfloat16
    field = pltpu.VMEM((nc, ny, nx), f32)
    n_ops = 4 * ny
    dma = pltpu.SemaphoreType.DMA
    any_spec = pl.BlockSpec(memory_space=pl.ANY)
    vmem_spec = pl.BlockSpec(memory_space=pltpu.VMEM)
    updated, gradient = pl.pallas_call(
        functools.partial(kernel, tuple(units), nz),
        out_shape=(field, field),
        in_specs=[any_spec] * 7,
        out_specs=(vmem_spec, vmem_spec),
        scratch_shapes=[pltpu.VMEM(a.shape, f32) for a in (stream_first, stream_second, wall_first, wall_second)] + [
            field, field, field, field,
            pltpu.VMEM((2 * nz, ny, nx), f32), pltpu.VMEM((nz, ny, nx), f32),
            pltpu.VMEM((nb // 2, 4 * blk, 2 * blk), bf16), pltpu.VMEM((nb // 2, 4 * blk, 2 * blk), bf16),
            pltpu.VMEM((ny, nx), bf16), pltpu.VMEM((ny, nx), bf16),
            pltpu.VMEM((nb // 2, ny, 4 * blk), f32),
            pltpu.VMEM((n_ops, 4 * ny), bf16), pltpu.VMEM((n_ops, 4 * ny), bf16),
            pltpu.VMEM((4 * ny, TILE), bf16), pltpu.VMEM((4 * ny, TILE), bf16),
        ] + [dma((nu,))] * 10 + [dma((nz,))] * 2 + [dma((nc,)), dma, dma((nu,)), dma((4,))],
        compiler_params=pltpu.CompilerParams(
            collective_id=0, has_side_effects=True, vmem_limit_bytes=48 << 20),
    )(
        adjoint.reshape(nc, ny, nx), base_flow.reshape(-1, ny, nx),
        stream_first, stream_second, wall_first, wall_second, forcing.reshape(nc, ny, nx),
    )
    hbm = jax.ShapeDtypeStruct((nc, ny, nx), f32)
    updated, gradient = pl.pallas_call(
        put,
        out_shape=(hbm, hbm),
        in_specs=[vmem_spec, vmem_spec],
        out_specs=(any_spec, any_spec),
        scratch_shapes=[dma((2, nc))],
        compiler_params=pltpu.CompilerParams(vmem_limit_bytes=1 << 20),
    )(updated, gradient)
    return updated.reshape(adjoint.shape), gradient.reshape(forcing.shape)


def put(updated, gradient, upd_out, grad_out, sem):
    copies = []
    for i, (src, dst) in enumerate(((updated, upd_out), (gradient, grad_out))):
        for c in range(src.shape[0]):
            copies.append(pltpu.make_async_copy(src.at[c], dst.at[c], sem.at[i, c]))
    for copy in copies:
        copy.start()
    for copy in copies:
        copy.wait()


def stream_terms(adj_field, stream_first, stream_second):
    block_count = stream_first.shape[0]
    block_size = stream_first.shape[1]
    blocks_view = adj_field.reshape(-1, block_count, block_size)
    first_sum = jnp.zeros(blocks_view.shape, jnp.float32)
    second_sum = jnp.zeros(blocks_view.shape, jnp.float32)
    for shift_count in range(block_count):
        shifted = jnp.roll(blocks_view, -shift_count, axis=1)
        first_sum = first_sum + jnp.einsum(
            "mpj,ij->mpi", shifted, stream_first[shift_count], precision=lax.Precision.HIGHEST
        )
        second_sum = second_sum + jnp.einsum(
            "mpj,ij->mpi", shifted, stream_second[shift_count], precision=lax.Precision.HIGHEST
        )
    return (first_sum.reshape(adj_field.shape), second_sum.reshape(adj_field.shape))


def local(adjoint, base_flow, stream_first, stream_second, wall_first, wall_second, forcing):
    adj_field = adjoint[0]
    base_speed = base_flow[0]
    x_first, x_second = stream_terms(adj_field, stream_first, stream_second)
    rhs_stream = viscosity * x_second + base_speed[0:1] * x_first
    lines = lax.all_to_all(adj_field, "row", split_axis=3, concat_axis=2, tiled=True)
    y_first = jnp.einsum("ky,fzyx->fzkx", wall_first, lines, precision=lax.Precision.HIGHEST)
    y_second = jnp.einsum("ky,fzyx->fzkx", wall_second, lines, precision=lax.Precision.HIGHEST)
    y_first, y_second = (y_first, y_second)
    y_first, y_second = (
        lax.all_to_all(y_first, "row", split_axis=2, concat_axis=3, tiled=True),
        lax.all_to_all(y_second, "row", split_axis=2, concat_axis=3, tiled=True),
    )
    rhs_wall = viscosity * y_second + base_speed[1:2] * y_first
    updated = adj_field + step_weight * (rhs_stream + rhs_wall)
    summed = lax.psum(updated, "ens")
    gradient = forcing * summed
    return (updated[None], gradient)


def solution(mesh):
    placed = (
        P("ens", None, "col", "row", None),
        P("ens", None, "col", "row", None),
        P(),
        P(),
        P(),
        P(),
        P(None, "col", "row", None),
    )
    small = mesh.shape["row"] == 4 and mesh.shape["ens"] == 2
    return jax.shard_map(
        fused if small else local,
        mesh=mesh,
        in_specs=placed,
        out_specs=(P("ens", None, "col", "row", None), P(None, "col", "row", None)),
        check_vma=False,
    )
```
